32 devices in a mesh: tg: 2 (over core), pw: 16 (over z, y, x).
Axes of the slice: x: 2, y: 2, z: 4, core: 2. Of those that a mesh axis runs over, the one named last changes fastest.
Arguments:
- coeffs: float32 [2, 8192, 256], P(None, ('tg', 'pw')), may hold values from -6 to 6
- g_place: int32 [8192], P(('tg', 'pw')), may hold values from 0 to 2047, as said below
- stick_column: int32 [512], P(('tg', 'pw')), may hold values from 0 to 16383, as said below
- potential: float32 [128, 128, 128], P(None, None, ('tg', 'pw')), may hold values from -1 to 3
Outputs:
- hpsi: float32 [2, 8192, 256], P(None, ('tg', 'pw'))
The draws below stay inside these ranges and needn't reach their ends.
Inputs may be any that keep to these rules, and one draw needn't show every extreme that they name: g_place[g] = s * 128 + z: s is a stick slot of the owner g // 256, z a frequency within 32 of zero taken modulo 128; no two plane waves of one owner share s and z; each owner uses its slots 0 up to some count between 4 and 16, every one of them, and some owner uses all 16. `stick_column`: all stick slots name different columns x * 128 + y; with x and y read as signed frequencies (taken modulo 128), x * x + y * y <= 32 ** 2.
All inputs are finite; a program needn't handle non-finite values.
Results may differ from the reference program's by a relative error of at most 0.009.
Values may be sent and summed in bfloat16 or wider, within the bound.
A program may use at most 256 MiB of HBM per device.

```python
import jax
import jax.numpy as jnp
from jax import lax

NR = 128
ZSPAN = 64
SLOT = 16
G_DEV = 256
BANDS = 256
G_TOTAL = 8192
STICKS = 512


def live_slots(key):
    owners = STICKS // SLOT
    random_part = SLOT // 4 + jax.random.randint(jax.random.fold_in(key, 11), (owners,), 0, SLOT - SLOT // 4 + 1)
    busiest = jax.random.randint(jax.random.fold_in(key, 12), (), 0, owners)
    return jnp.where(jnp.arange(owners) == busiest, SLOT, random_part)


def draw_g_place(key, part):
    owners = STICKS // SLOT
    cell_count = SLOT * ZSPAN
    live_count = live_slots(key)
    position = jnp.arange(cell_count, dtype=jnp.int32)
    slot_of = position // ZSPAN
    random_part = jax.random.randint(jax.random.fold_in(key, 13), (owners, cell_count), 0, 2 ** 20)
    scores = random_part * cell_count + position[None, :]
    scores = jnp.where(position[None, :] % ZSPAN == 0, 2 ** 30 + position[None, :], scores)
    scores = jnp.where(slot_of[None, :] < live_count[:, None], scores, -1 - position[None, :])
    chosen = lax.top_k(scores, G_DEV)[1]
    frequency = chosen % ZSPAN - ZSPAN // 2
    placed = chosen // ZSPAN * NR + jnp.mod(frequency, NR)
    return placed.reshape(G_TOTAL).astype(jnp.int32)


def draw_stick_column(key, part):
    radius = ZSPAN // 2
    side_length = ZSPAN + 1
    cell_count = side_length * side_length
    position = jnp.arange(cell_count, dtype=jnp.int32)
    x_signed = position // side_length - radius
    y_signed = position % side_length - radius
    inside = x_signed * x_signed + y_signed * y_signed <= radius * radius
    random_part = jax.random.randint(jax.random.fold_in(key, 21), (cell_count,), 0, 2 ** 16)
    scores = jnp.where(inside, random_part * cell_count + position, -1 - position)
    chosen = lax.top_k(scores, STICKS)[1]
    x_index = jnp.mod(x_signed[chosen], NR)
    y_index = jnp.mod(y_signed[chosen], NR)
    return (x_index * NR + y_index).astype(jnp.int32)


def shard_levels(stream_key, extent, shards, low, high):
    def one(axis_at, parts):
        heights = jax.random.uniform(jax.random.fold_in(jax.random.fold_in(stream_key, 6), axis_at), (parts,), jnp.float32, low / len(shards), high / len(shards))
        return jnp.repeat(jnp.exp(heights), extent[axis_at] // parts).reshape((-1,) + (1,) * (len(extent) - axis_at - 1))

    level = one(*shards[0])
    for cut in shards[1:]:
        level = level * one(*cut)
    return level


def bell_draw(stream_key, shape, deviation, most, shards=(), kind=jnp.bfloat16):
    result = deviation * jax.random.normal(stream_key, shape, jnp.float32)
    if shards:
        result = result * shard_levels(stream_key, shape, shards, -0.22, 0.18)
    return jnp.clip(result, -most, most).astype(kind)


def setup_inputs(seed: int = 0) -> dict:
    seeds = jax.random.split(jax.random.key(seed), 5)
    return {
        "coeffs": bell_draw(seeds[0], (2, G_TOTAL, BANDS), 1.0, 6.0, ((1, 32),), jnp.float32),
        "g_place": draw_g_place(jax.random.fold_in(seeds[4], 71), 0),
        "stick_column": draw_stick_column(jax.random.fold_in(seeds[4], 71), 0),
        "potential": jnp.clip(-1.0 + 4.0 * jax.random.uniform(seeds[3], (NR, NR, NR), jnp.float32) ** shard_levels(seeds[3], (NR, NR, NR), ((2, 32),), -0.2, 0.2), -1.0, 3.0),
    }


def phase_table(left_index, right_index, sign_value, modulus):
    product = (left_index[:, None] * right_index[None, :]) % modulus
    angles = (2.0 * jnp.pi / modulus) * product.astype(jnp.float32)
    cosine = jnp.cos(angles)
    sine_part = sign_value * jnp.sin(angles)
    upper_row = jnp.stack([cosine, sine_part])
    lower_row = jnp.stack([-sine_part, cosine])
    return jnp.stack([upper_row, lower_row])


def plane_pass(lattice, volume, forward, inverse):
    ahead = forward.astype(jnp.float32)
    behind = inverse.astype(jnp.float32)
    partial_value = jnp.einsum('cxypb,cdyk->dxkpb', lattice.astype(jnp.float32), ahead).astype(jnp.bfloat16)
    psi_field = jnp.einsum('cxypb,cdxk->dkypb', partial_value.astype(jnp.float32), ahead)
    weighted = (psi_field * volume[None, :, :, :, None]).astype(jnp.bfloat16)
    reverse_half = jnp.einsum('cxypb,cdyk->dxkpb', weighted.astype(jnp.float32), behind).astype(jnp.bfloat16)
    return jnp.einsum('cxypb,cdxk->dkypb', reverse_half.astype(jnp.float32), behind)


def reference(coeffs, g_place, stick_column, potential):
    frequency = jnp.arange(NR, dtype=jnp.int32)
    forward = phase_table(frequency, frequency, 1.0, NR).astype(jnp.bfloat16)
    inverse = phase_table(frequency, frequency, -1.0, NR).astype(jnp.bfloat16)
    ahead_table = phase_table(frequency, frequency, 1.0, NR)
    return_table = phase_table(frequency, frequency, -1.0, NR)
    holder = (jnp.arange(G_TOTAL, dtype=jnp.int32) // G_DEV).astype(jnp.int32)
    flat_index = (holder * (SLOT * NR) + g_place).astype(jnp.int32)
    factor = 1.0 / NR ** 3

    def one_band(band_values):
        placed = jnp.zeros((2, STICKS * NR), jnp.float32).at[:, flat_index].add(band_values)
        placed = placed.reshape(2, STICKS, NR)
        sticks = jnp.einsum('csz,cdzk->dsk', placed, ahead_table, precision=lax.Precision.HIGHEST).astype(jnp.bfloat16)
        lattice = jnp.zeros((2, NR * NR, NR), jnp.bfloat16).at[:, stick_column].set(sticks)
        real_image = plane_pass(lattice.reshape(2, NR, NR, NR, 1), potential, forward, inverse)
        picked = real_image.reshape(2, NR * NR, NR)[:, stick_column].astype(jnp.bfloat16)
        spectra = jnp.einsum('csz,cdzk->dsk', picked.astype(jnp.float32), return_table, precision=lax.Precision.HIGHEST)
        return spectra.reshape(2, STICKS * NR)[:, flat_index] * factor

    stacked = lax.map(one_band, jnp.transpose(coeffs, (2, 0, 1)))
    return jnp.transpose(stacked, (1, 2, 0))
```

```python
import jax
import jax.numpy as jnp
from jax import lax
from jax.sharding import PartitionSpec as P

NR = 128
ZSPAN = 64


def phase_table(left_index, right_index, sign_value, modulus):
    product = left_index[:, None] * right_index[None, :] % modulus
    angles = 2.0 * jnp.pi / modulus * product.astype(jnp.float32)
    cosine = jnp.cos(angles)
    sine_part = sign_value * jnp.sin(angles)
    upper_row = jnp.stack([cosine, sine_part])
    lower_row = jnp.stack([-sine_part, cosine])
    return jnp.stack([upper_row, lower_row])


def box_selectors(column_order):
    half_span = ZSPAN // 2
    box_side = ZSPAN + 1
    x_index = column_order // NR
    y_index = column_order % NR
    x_box = jnp.where(x_index > NR // 2, x_index - NR, x_index) + half_span
    y_box = jnp.where(y_index > NR // 2, y_index - NR, y_index) + half_span
    cells = jnp.arange(box_side * box_side, dtype=jnp.int32)
    forward_select = (cells[:, None] == (y_box * box_side + x_box)[None, :]).astype(jnp.bfloat16)
    backward_select = (cells[:, None] == (x_box * box_side + y_box)[None, :]).astype(jnp.bfloat16)
    return (forward_select, backward_select)


def box_tables():
    box_side = ZSPAN + 1
    frequency = jnp.arange(NR, dtype=jnp.int32)
    box_freq = jnp.mod(jnp.arange(box_side, dtype=jnp.int32) - ZSPAN // 2, NR)
    ahead = phase_table(box_freq, frequency, 1.0, NR).astype(jnp.bfloat16)
    behind = phase_table(frequency, box_freq, -1.0, NR).astype(jnp.bfloat16)
    return (ahead, behind)


def one_plane(flat, volume, selectors, ahead, behind):
    forward_select, backward_select = selectors
    box_side = ZSPAN + 1
    band_count = flat.shape[2]
    lattice = jnp.stack(
        [
            jnp.dot(forward_select, flat[part_index], preferred_element_type=jnp.float32)
            .astype(jnp.bfloat16)
            .reshape(box_side, box_side, band_count)
            for part_index in range(2)
        ]
    )
    partial_value = jnp.einsum(
        "cdyk,cyxm->dkxm", ahead, lattice, preferred_element_type=jnp.float32
    ).astype(jnp.bfloat16)
    psi_field = jnp.einsum(
        "cdxr,ckxm->drkm", ahead, partial_value, preferred_element_type=jnp.float32
    )
    weighted = (psi_field * volume[None, :, :, None]).astype(jnp.bfloat16)
    reverse_half = jnp.einsum(
        "cdyq,cxym->dqxm", behind, weighted, preferred_element_type=jnp.float32
    ).astype(jnp.bfloat16)
    real_image = jnp.einsum(
        "cdxq,cyxm->dqym", behind, reverse_half, preferred_element_type=jnp.float32
    )
    boxed = real_image.astype(jnp.bfloat16).reshape(2, box_side * box_side, band_count)
    picked = jnp.stack(
        [
            jnp.einsum(
                "qs,qm->sm", backward_select, boxed[part_index], preferred_element_type=jnp.float32
            )
            for part_index in range(2)
        ]
    )
    return picked.astype(jnp.bfloat16)


def plane_pass(received, selectors, volume, ahead, behind):
    def step(carry, item):
        return carry, one_plane(item[0], item[1], selectors, ahead, behind)

    planes = (jnp.moveaxis(received, 2, 0), jnp.moveaxis(volume, 2, 0))
    return jnp.moveaxis(lax.scan(step, None, planes)[1], 0, 2)


def spread(shared, indices, slot_total):
    band_count = shared.shape[2]
    selector = (indices[:, None] == jnp.arange(slot_total * NR, dtype=jnp.int32)[None, :]).astype(
        jnp.float32
    )
    placed = jnp.einsum("gq,cgb->cqb", selector, shared, precision=lax.Precision.HIGHEST)
    return (selector, placed.reshape(2, slot_total, NR, band_count))


def ahead_sticks(placed, plane_of):
    frequency = jnp.arange(NR, dtype=jnp.int32)
    ahead_table = phase_table(frequency, plane_of, 1.0, NR)
    sticks = jnp.einsum("cszb,cdzk->dskb", placed, ahead_table, precision=lax.Precision.HIGHEST)
    return sticks.astype(jnp.bfloat16)


def finish(arrived, plane_of, selector):
    frequency = jnp.arange(NR, dtype=jnp.int32)
    return_table = phase_table(plane_of, frequency, -1.0, NR)
    spectra = jnp.einsum(
        "cszb,cdzk->dskb",
        arrived.astype(jnp.float32),
        return_table,
        precision=lax.Precision.HIGHEST,
    )
    band_count = arrived.shape[3]
    picked = jnp.einsum(
        "gq,cqb->cgb", selector, spectra.reshape(2, -1, band_count), precision=lax.Precision.HIGHEST
    )
    return picked * (1.0 / NR**3)


def body(coeffs, g_place, stick_column, potential):
    owners = lax.axis_size(("tg", "pw"))
    copies = jnp.broadcast_to(stick_column[None], (owners,) + stick_column.shape)
    columns = lax.all_to_all(
        copies, ("tg", "pw"), split_axis=0, concat_axis=0, tiled=True
    ).reshape(-1)
    ahead, behind = box_tables()
    slot_width = stick_column.shape[0]
    plane_of = jnp.arange(NR, dtype=jnp.int32)
    selector, placed = spread(coeffs, g_place, slot_width)
    sticks = ahead_sticks(placed, plane_of)
    selectors = box_selectors(columns)
    returned = plane_pass(
        lax.all_to_all(sticks, ("tg", "pw"), split_axis=2, concat_axis=1, tiled=True),
        selectors,
        potential,
        ahead,
        behind,
    )
    arrived = lax.all_to_all(returned, ("tg", "pw"), split_axis=1, concat_axis=2, tiled=True)
    return finish(arrived, plane_of, selector)


def solution(mesh):
    placed = (
        P(None, ("tg", "pw"), None),
        P(("tg", "pw")),
        P(("tg", "pw")),
        P(None, None, ("tg", "pw")),
    )
    return jax.shard_map(
        body, mesh=mesh, in_specs=placed, out_specs=P(None, ("tg", "pw"), None), check_vma=False
    )
```
